32 devices in a mesh: dp: 8 (over y, x, core), mp: 4 (over z).
Axes of the slice: x: 2, y: 2, z: 4, core: 2. Of those that a mesh axis runs over, the one named last changes fastest.
Arguments:
- token_block: int32 [8192, 1], P(('dp', 'mp')), may hold values from 0 to 31; in each aligned block of 256 rows (0 to 255, 256 to 511, ...) at most 16 rows name the same one
- token_offset: int32 [8192], P(('dp', 'mp')), may hold values from 0 to 15663
- lengths: int32 [128], P(('dp', 'mp')), may hold values from 1 to 64, as said below
- group_counts: int32 [109], replicated, may hold values from 1 to 16, 128 in all
- table: bfloat16 [501248, 768], P(('dp', 'mp')), may hold values from -6 to 6
- weight_qkv: bfloat16 [768, 2304], P(None, 'mp'), may hold values from -0.21875 to 0.21875
- bias_query: bfloat16 [768], P('mp'), may hold values from -2 to 2
- bias_value: bfloat16 [768], P('mp'), may hold values from -2 to 2
- weight_out: bfloat16 [768, 768], P('mp'), may hold values from -0.875 to 0.875
- bias_out: bfloat16 [768], replicated, may hold values from -2 to 2
- gain_one: bfloat16 [768], replicated, may hold values from 0.5 to 1.5
- shift_one: bfloat16 [768], replicated, may hold values from -2 to 2
- weight_in: bfloat16 [768, 3072], P(None, 'mp'), may hold values from -0.21875 to 0.21875
- bias_in: bfloat16 [3072], P('mp'), may hold values from -2 to 2
- weight_down: bfloat16 [3072, 768], P('mp'), may hold values from -0.15625 to 0.15625
- bias_down: bfloat16 [768], replicated, may hold values from -2 to 2
- gain_two: bfloat16 [768], replicated, may hold values from 0.5 to 1.5
- shift_two: bfloat16 [768], replicated, may hold values from -2 to 2
- cotangent: bfloat16 [8192, 768], P(('dp', 'mp')), may hold values from -6 to 6
Outputs:
- activations: bfloat16 [8192, 768], P(('dp', 'mp'))
- grad_table: float32 [501248, 768], P(('dp', 'mp'))
- grad_weight_qkv: float32 [768, 2304], P(None, 'mp')
- grad_bias_query: float32 [768], P('mp')
- grad_bias_value: float32 [768], P('mp')
- grad_weight_out: float32 [768, 768], P('mp')
- grad_bias_out: float32 [768], replicated
- grad_gain_one: float32 [768], replicated
- grad_shift_one: float32 [768], replicated
- grad_weight_in: float32 [768, 3072], P(None, 'mp')
- grad_bias_in: float32 [3072], P('mp')
- grad_weight_down: float32 [3072, 768], P('mp')
- grad_bias_down: float32 [768], replicated
- grad_gain_two: float32 [768], replicated
- grad_shift_two: float32 [768], replicated
The draws below stay inside these ranges and needn't reach their ends.
Inputs may be any that keep to these rules, and one draw needn't show every extreme that they name: `token_block`: among the rows of one device, at most 16 tokens name the same block. `lengths`: positions from a sentence's length on are padding. `group_counts`: the counts sum to 128.
All inputs are finite; a program needn't handle non-finite values.
Results may differ from the reference program's by a relative error of at most 0.02.
Values may be sent and summed in bfloat16 or wider, within the bound.
A program may use at most 192 MiB of HBM per device.

```python
import math
import jax
import jax.numpy as jnp
import numpy as np
from jax import lax

D = 768
NH = 12
HD = 64
FF = 3072
VOCAB = 501248
SEQ = 64
NGROUPS = 109
TOK_DEV = 256
SENTENCES = 128
TOKENS = 8192
ROWS_DEV = 15664
CAP = 16
GROUP_MOST = 16
DEVICES = 32


def draw_lengths(key, part):
    sent_index = jnp.arange(SENTENCES, dtype=jnp.int32)
    low_ceiling = SEQ // 4
    ceiling = 1 + low_ceiling + (SEQ - 1 - low_ceiling) * sent_index // max(SENTENCES - 1, 1)
    noise_bits = jax.random.randint(key, (SENTENCES,), 0, 1 << 20, dtype=jnp.int32)
    drawn_len = 1 + noise_bits % ceiling
    drawn_len = jnp.where(sent_index == SENTENCES - 1, SEQ, drawn_len)
    return jnp.where(sent_index == 0, 1, drawn_len).astype(jnp.int32)


def with_ends(values, stream_key, smallest, high):
    longest = values.shape.index(max(values.shape))
    spots = []
    for shift in (0, 1):
        where = [jax.random.randint(jax.random.fold_in(stream_key, axis), (), 0, length) for axis, length in enumerate(values.shape)]
        where[longest] = (where[longest] + shift) % values.shape[longest]
        spots.append(tuple(where))
    return values.at[spots[0]].set(smallest).at[spots[1]].set(high)


def shard_levels(rng, shape, shards, least, high):
    def one(position, shards_of):
        heights = jax.random.uniform(jax.random.fold_in(jax.random.fold_in(rng, 6), position), (shards_of,), jnp.float32, least / len(shards), high / len(shards))
        return jnp.repeat(jnp.exp(heights), shape[position] // shards_of).reshape((-1,) + (1,) * (len(shape) - position - 1))

    level = one(*shards[0])
    for cut in shards[1:]:
        level = level * one(*cut)
    return level


def split_up(amount, total, most, skew):
    weights = [(1 << 20) // math.isqrt(rank ** skew) + 1 for rank in range(2, amount + 1)]
    surplus, holding = total - most - (amount - 1), [1] * (amount - 1)
    while surplus > 0:
        free = [i for i in range(amount - 1) if holding[i] < most]
        whole, left = sum([weights[i] for i in free]), surplus
        for i in free:
            extra = min(most - holding[i], max(1, left * weights[i] // whole), surplus)
            holding[i] = holding[i] + extra
            surplus = surplus - extra
    return np.array([most] + holding)


def ragged(key, number_of, total, bound, skew):
    if number_of == 2:
        one = jax.random.randint(key, (), max(1, total - bound), min(bound, total - 1) + 1)
        return jnp.stack([one, total - one])
    sizes = jnp.asarray(split_up(number_of, total, bound, skew), jnp.int32)
    couples = (number_of - 1) // 2
    giver, sink = sizes[1:1 + 2 * couples:2], sizes[2:2 + 2 * couples:2]
    slack = jnp.minimum(giver - 1, bound - sink)
    shifted = jax.random.randint(jax.random.fold_in(key, 1), (couples,), 0, 1 << 20) % (slack + 1)
    sizes = sizes.at[1:1 + 2 * couples:2].set(giver - shifted).at[2:2 + 2 * couples:2].set(sink + shifted)
    return sizes[jax.random.permutation(jax.random.fold_in(key, 2), number_of)]


def assign_block(own_key, own, number, rows, count, top, reach, skew):
    sequence = jax.random.permutation(own_key, count)
    heavy_load, ordinary = load_shares(count, rows * top, reach, skew, True), load_shares(count, rows * top, reach, skew, False)
    places = jnp.arange(count)

    def named(tallies, rotation):
        used = int((tallies > 0).sum())
        fixed = max(1, used // 4)
        passed = fixed + (places - fixed + rotation * (used - fixed)) % max(1, count - fixed)
        return jnp.zeros((count,), jnp.int32).at[sequence[jnp.where(places < fixed, places, passed)]].set(jnp.asarray(tallies, jnp.int32))

    tallies = jnp.where(number % 4 == 0, named(heavy_load, number // 4), named(ordinary, number - number // 4 - 1))
    mixed = jax.random.permutation(jax.random.fold_in(own, 3), count)
    source_of, receiver = mixed[0:count // 2 * 2:2], mixed[1:count // 2 * 2:2]
    room = jnp.minimum(tallies[source_of] - 1, reach - tallies[receiver]) // 2
    room = jnp.where((source_of == sequence[0]) | (receiver == sequence[0]) | (tallies[receiver] == 0), 0, jnp.maximum(room, 0))
    passed = jax.random.randint(jax.random.fold_in(own, 4), (count // 2,), 0, 1 << 20) % (room + 1)
    tallies = tallies.at[source_of].add(-passed).at[receiver].add(passed)
    items = jnp.searchsorted(jnp.cumsum(tallies), jnp.arange(rows * top), side="right").astype(jnp.int32)
    grid = items.reshape(top, rows).T
    grid = grid[jax.random.permutation(jax.random.fold_in(own, 1), rows)]
    rotation = jax.random.randint(jax.random.fold_in(own, 2), (rows, 1), 0, top)
    return jnp.take_along_axis(grid, (jnp.arange(top)[None, :] + rotation) % top, axis=1)


def load_shares(amount, total, bound, skew, full):
    portions = [(1 << 20) // math.isqrt(rank ** skew) + 1 for rank in range(1, amount + 1)]
    largest = bound if full else min(bound, max(-(-total // amount), total * portions[0] // sum(portions)))
    least = 1 if total - largest >= amount - 1 else 0
    given, rest = [largest] + [least] * (amount - 1), total - largest - least * (amount - 1)
    while rest > 0:
        free = [i for i in range(1, amount) if given[i] < largest] or [i for i in range(1, amount) if given[i] < bound]
        whole, left = sum([portions[i] for i in free]), rest
        for i in free:
            addition = min(bound - given[i], max(1, left * portions[i] // whole), rest)
            given[i] = given[i] + addition
            rest = rest - addition
    return np.array(given)


def normal_values(own_key, dims, width, limit, cuts=(), kind=jnp.bfloat16):
    array = width * jax.random.normal(own_key, dims, jnp.float32)
    if cuts:
        array = array * shard_levels(own_key, dims, cuts, -0.22, 0.18)
    return jnp.clip(array, -limit, limit).astype(kind)


def setup_inputs(seed: int = 0) -> dict:
    key_list = jax.random.split(jax.random.key(seed), 20)
    token_block_keys = jax.random.split(jax.random.fold_in(key_list[0], 1), TOKENS // TOK_DEV)
    token_block_turns = jax.random.permutation(jax.random.fold_in(key_list[0], 3), TOKENS // TOK_DEV)
    token_block = jax.vmap(lambda own, number: assign_block(jax.random.fold_in(key_list[0], 2), own, number, TOK_DEV, DEVICES, 1, CAP, 1))(token_block_keys, token_block_turns).reshape((TOKENS, 1))
    token_offset = with_ends(jax.random.randint(key_list[1], (TOKENS,), 0, ROWS_DEV), jax.random.fold_in(key_list[1], 1), 0, ROWS_DEV - 1).astype(jnp.int32)
    lengths = draw_lengths(jax.random.fold_in(key_list[19], 71), 0)
    group_counts = ragged(key_list[3], NGROUPS, SENTENCES, GROUP_MOST, 2).astype(jnp.int32)
    table = normal_values(key_list[4], (VOCAB, D), 1.0, 6.0, ((0, 32),))
    weight_qkv = normal_values(key_list[5], (D, 3 * D), D ** -0.5, 0.21875, ((1, 4),))
    bias_query = normal_values(key_list[6], (D,), 0.3, 2.0, ((0, 4),))
    bias_value = normal_values(key_list[7], (D,), 0.3, 2.0, ((0, 4),))
    weight_out = normal_values(key_list[8], (D, D), (D // 16) ** -0.5, 0.875, ((0, 4),))
    bias_out = normal_values(key_list[9], (D,), 0.3, 2.0)
    gain_one = jnp.clip(1.0 + 0.1 * jax.random.normal(key_list[10], (D,), jnp.float32), 0.5, 1.5).astype(jnp.bfloat16)
    shift_one = normal_values(key_list[11], (D,), 0.3, 2.0)
    weight_in = normal_values(key_list[12], (D, FF), D ** -0.5, 0.21875, ((1, 4),))
    bias_in = normal_values(key_list[13], (FF,), 0.3, 2.0, ((0, 4),))
    weight_down = normal_values(key_list[14], (FF, D), (FF // 2) ** -0.5, 0.15625, ((0, 4),))
    bias_down = normal_values(key_list[15], (D,), 0.3, 2.0)
    gain_two = jnp.clip(1.0 + 0.1 * jax.random.normal(key_list[16], (D,), jnp.float32), 0.5, 1.5).astype(jnp.bfloat16)
    shift_two = normal_values(key_list[17], (D,), 0.3, 2.0)
    cotangent = normal_values(key_list[18], (TOKENS, D), 1.0, 6.0, ((0, 32),))
    return {"token_block": token_block, "token_offset": token_offset, "lengths": lengths, "group_counts": group_counts, "table": table, "weight_qkv": weight_qkv, "bias_query": bias_query, "bias_value": bias_value, "weight_out": weight_out, "bias_out": bias_out, "gain_one": gain_one, "shift_one": shift_one, "weight_in": weight_in, "bias_in": bias_in, "weight_down": weight_down, "bias_down": bias_down, "gain_two": gain_two, "shift_two": shift_two, "cotangent": cotangent}


@jax.custom_vjp
def low(v):
    return lax.optimization_barrier(v.astype(jnp.bfloat16)).astype(jnp.float32)

@jax.custom_vjp
def low_back(v):
    return v

def low_keep(v):
    return (low(v), None)

def low_pass(kept, grad):
    return (grad,)

def back_keep(v):
    return (v, None)

def back_low(kept, grad):
    return (low(grad),)
low.defvjp(low_keep, low_pass)
low_back.defvjp(back_keep, back_low)
highest = lax.Precision.HIGHEST
eps_norm = 1e-12

def layer_norm(hidden, gain_vec, shift_vec):
    row_mean = lax.optimization_barrier(jnp.mean(hidden, axis=-1, keepdims=True))
    centred = hidden - row_mean
    variance = lax.optimization_barrier(jnp.mean(centred * centred, axis=-1, keepdims=True))
    return centred * lax.rsqrt(variance + eps_norm) * gain_vec + shift_vec

def forward(embedded, sent_lengths, weight_qkv, bias_query, bias_value, weight_out, bias_out, gain_one, shift_one, weight_in, bias_in, weight_down, bias_down, gain_two, shift_two):
    sent_count = sent_lengths.shape[0]
    mixed_qkv = jnp.dot(embedded, weight_qkv, precision=highest).reshape(sent_count, SEQ, NH, 3, HD)
    queries = low_back(low(mixed_qkv[:, :, :, 0, :] + bias_query.reshape(NH, HD)))
    key_rows = low_back(low(mixed_qkv[:, :, :, 1, :]))
    value_rows = low_back(low(mixed_qkv[:, :, :, 2, :] + bias_value.reshape(NH, HD)))
    scores = low_back(jnp.einsum('sqhe,skhe->shqk', queries, key_rows, precision=highest) * 0.125)
    key_valid = jnp.arange(SEQ)[None, :] < sent_lengths[:, None]
    scores = jnp.where(key_valid[:, None, None, :], scores, -1e+30)
    attn_probs = low(jax.nn.softmax(scores, axis=-1))
    context = low_back(low(jnp.einsum('shqk,skhe->sqhe', attn_probs, value_rows, precision=highest)))
    attn_out = low_back(jnp.dot(context.reshape(-1, D), weight_out, precision=highest))
    first_out = layer_norm(embedded + attn_out + bias_out, gain_one, shift_one)
    hidden_pre = low_back(jnp.dot(low(first_out), weight_in, precision=highest) + bias_in)
    hidden_act = low(jax.nn.gelu(hidden_pre, approximate=False))
    down_out = low_back(jnp.dot(hidden_act, weight_down, precision=highest))
    return layer_norm(first_out + down_out + bias_down, gain_two, shift_two)

def reference(token_block, token_offset, lengths, group_counts, table, weight_qkv, bias_query, bias_value, weight_out, bias_out, gain_one, shift_one, weight_in, bias_in, weight_down, bias_down, gain_two, shift_two, cotangent):
    params = tuple((part.astype(jnp.float32) for part in (weight_qkv, bias_query, bias_value, weight_out, bias_out, gain_one, shift_one, weight_in, bias_in, weight_down, bias_down, gain_two, shift_two)))
    token_rows = (token_block[:, 0] * ROWS_DEV + token_offset).astype(jnp.int32)
    embedded = table[token_rows].astype(jnp.float32)
    counts_float = group_counts.astype(jnp.float32)
    offsets = jnp.cumsum(group_counts) - group_counts
    sent_index = jnp.arange(SENTENCES, dtype=jnp.int32)
    member = (sent_index[:, None] >= offsets[None, :]) & (sent_index[:, None] < (offsets + group_counts)[None, :])
    group_weight = SENTENCES / (NGROUPS * counts_float)
    sent_weight = lax.optimization_barrier(jnp.sum(jnp.where(member, group_weight[None, :], jnp.float32(0.0)), axis=1))
    token_live = (jnp.arange(SEQ)[None, :] < lengths[:, None]).astype(jnp.float32)
    row_weight = (token_live * sent_weight[:, None]).reshape(TOKENS)
    grad_final = row_weight[:, None] * cotangent.astype(jnp.float32)
    block_sent = min(64, SENTENCES)
    block_count = SENTENCES // block_sent
    emb_blocks = embedded.reshape(block_count, block_sent * SEQ, D)
    len_blocks = lengths.reshape(block_count, block_sent)
    grad_blocks = grad_final.reshape(block_count, block_sent * SEQ, D)
    zero_grads = tuple((jnp.zeros_like(part) for part in params))

    def scan_step(carried, block_items):
        emb_blk, len_blk, grad_blk = block_items
        layer_out, pullback = jax.vjp(lambda emb_in, *weights: forward(emb_in, len_blk, *weights), emb_blk, *params)
        gradients = pullback(grad_blk)
        return (tuple((total_part + new_part for total_part, new_part in zip(carried, gradients[1:]))), (layer_out, gradients[0]))
    summed, (outputs, grad_emb) = lax.scan(scan_step, zero_grads, (emb_blocks, len_blocks, grad_blocks))
    factor = lax.rsqrt(jnp.sum(lengths).astype(jnp.float32))
    grad_table = jnp.zeros((VOCAB, D), jnp.float32).at[token_rows].add(grad_emb.reshape(TOKENS, D)) * factor
    activations = outputs.reshape(TOKENS, D).astype(jnp.bfloat16)
    scaled = tuple((part * factor for part in summed))
    return (activations, grad_table, scaled[0], scaled[1], scaled[2], scaled[3], scaled[4], scaled[5], scaled[6], scaled[7], scaled[8], scaled[9], scaled[10], scaled[11], scaled[12])
```

```python
from functools import partial

import jax
import jax.numpy as jnp
from jax import lax
from jax.experimental import pallas as pl
from jax.experimental.pallas import tpu as pltpu
from jax.sharding import PartitionSpec as P

HD = 64
SEQ = 64
EPS = 1e-12
MESH = pl.DeviceIdType.MESH
F32 = jnp.float32
BF16 = jnp.bfloat16

INNER = 8
BLOCKS = 3


def position():
    d = lax.axis_index("dp")
    m = lax.axis_index("mp")
    core = lax.rem(d, 2)
    first = 4 - 2 * core
    second = 2 + 2 * core
    return d, m, first, second


def flip(d, bit):
    return d + bit - 2 * bit * lax.rem(lax.div(d, bit), 2)


def enter(d, m, mp):
    barrier = pltpu.get_barrier_semaphore()
    peers = [(flip(d, bit), m) for bit in (1, 2, 4)] + [(d, lax.rem(m + k, mp)) for k in range(1, mp)]
    for peer in peers:
        pl.semaphore_signal(barrier, inc=1, device_id=peer, device_id_type=MESH)
    pl.semaphore_wait(barrier, len(peers))


def remote(src, dst, send, recv, peer):
    return pltpu.make_async_remote_copy(
        src_ref=src, dst_ref=dst, send_sem=send, recv_sem=recv, device_id=peer, device_id_type=MESH
    )


def gather_kernel(mp, own_ref, out_ref, send, recv, own_sem):
    d, m, first, second = position()
    enter(d, m, mp)
    s = lax.rem(d, INNER)
    s1 = flip(s, first)
    s2 = flip(s, second)
    s3 = flip(s1, second)
    for a in range(BLOCKS):
        pltpu.make_async_copy(own_ref.at[a], out_ref.at[a, m], own_sem.at[a]).start()
    z_copies = []
    for a in range(BLOCKS):
        for k in range(1, mp):
            copy = remote(
                own_ref.at[a, s], out_ref.at[a, m, s], send.at[a, k, 0], recv.at[a, mp - k, 0], (d, lax.rem(m + k, mp))
            )
            copy.start()
            z_copies.append(copy)

    def hop(a, k, piece, slot, bit):
        ref = out_ref.at[a, lax.rem(m + k, mp), piece]
        return remote(ref, ref, send.at[a, k, slot], recv.at[a, k, slot], (flip(d, bit), m))

    units = [(a, k) for a in range(BLOCKS) for k in range(1, mp)]
    sent = []

    def go(copy):
        copy.start()
        sent.append(copy)

    def wait_z(a, k):
        ref = out_ref.at[a, lax.rem(m + k, mp), s]
        remote(ref, ref, send.at[a, k, 0], recv.at[a, k, 0], (d, lax.rem(m + k, mp))).wait_recv()

    for t in range(len(units) + 3):
        if t < len(units):
            a, k = units[t]
            wait_z(a, k)
            go(hop(a, k, s, 1, first))
            go(hop(a, k, s, 2, second))
            go(hop(a, k, s, 4, 1))
        if 0 <= t - 1 < len(units):
            a, k = units[t - 1]
            hop(a, k, s1, 1, first).wait_recv()
            go(hop(a, k, s1, 3, second))
            go(hop(a, k, s1, 5, 1))
        if 0 <= t - 2 < len(units):
            a, k = units[t - 2]
            hop(a, k, s2, 2, second).wait_recv()
            go(hop(a, k, s2, 6, 1))
            hop(a, k, s3, 3, second).wait_recv()
            go(hop(a, k, s3, 7, 1))
        if 0 <= t - 3 < len(units):
            a, k = units[t - 3]
            for slot, piece in ((4, s), (5, s1), (6, s2), (7, s3)):
                hop(a, k, flip(piece, 1), slot, 1).wait_recv()
    for copy in z_copies + sent:
        copy.wait_send()
    for a in range(BLOCKS):
        pltpu.make_async_copy(own_ref.at[a], out_ref.at[a, m], own_sem.at[a]).wait()


def gather_weights(own, mp):
    _, inner, rows, width = own.shape
    return pl.pallas_call(
        partial(gather_kernel, mp),
        out_shape=jax.ShapeDtypeStruct((BLOCKS, mp, inner, rows, width), BF16),
        in_specs=[pl.BlockSpec(memory_space=pltpu.VMEM)],
        out_specs=pl.BlockSpec(memory_space=pltpu.VMEM),
        scratch_shapes=[
            pltpu.SemaphoreType.DMA((BLOCKS, mp, 8)),
            pltpu.SemaphoreType.DMA((BLOCKS, mp, 8)),
            pltpu.SemaphoreType.DMA((BLOCKS,)),
        ],
        compiler_params=pltpu.CompilerParams(
            collective_id=0, has_side_effects=True, vmem_limit_bytes=60 * 1024 * 1024
        ),
    )(own)


def reduce_kernel(mp, grad_ref, out_ref, near, mid, far, line, send, recv):
    d, m, first, second = position()
    enter(d, m, mp)
    s = lax.rem(d, INNER)
    s1 = flip(s, first)
    s2 = flip(s, second)
    s3 = flip(s1, second)
    mine = (s, s1, s2, s3)
    other = tuple(flip(piece, 1) for piece in (s, s2, s1, s3))
    sent = []

    def go(copy):
        copy.start()
        sent.append(copy)

    units = [(a, k) for a in range(BLOCKS) for k in (*range(1, mp), 0)]

    def add(into, more):
        into[...] = (into[...].astype(F32) + more[...].astype(F32)).astype(BF16)

    def near_copy(a, k, i, owner):
        return remote(
            grad_ref.at[a, owner, other[i]], near.at[a, k, i], send.at[a, k, i], recv.at[a, k, i], (flip(d, 1), m)
        )

    def mid_copy(a, k, i):
        return remote(
            near.at[a, k, 2 + i], mid.at[a, k, i], send.at[a, k, 4 + i], recv.at[a, k, 4 + i], (flip(d, second), m)
        )

    def far_copy(a, k):
        return remote(mid.at[a, k, 1], far.at[a, k], send.at[a, k, 6], recv.at[a, k, 6], (flip(d, first), m))

    def line_copy(a, k, owner):
        return remote(far.at[a, k], line.at[a, mp - k], send.at[a, k, 7], recv.at[a, mp - k, 7], (d, owner))

    def spread(a, i, piece, bit):
        ref = out_ref.at[a, piece]
        return remote(ref, ref, send.at[a, mp, i], recv.at[a, mp, i], (flip(d, bit), m))

    for a, k in units:
        for i in (2, 3, 0, 1):
            go(near_copy(a, k, i, lax.rem(m + k, mp)))
    for t in range(len(units) + 2):
        if t < len(units):
            a, k = units[t]
            owner = lax.rem(m + k, mp)
            for i in (2, 3, 0, 1):
                near_copy(a, k, i, owner).wait_recv()
                add(near.at[a, k, i], grad_ref.at[a, owner, mine[i]])
                if i >= 2:
                    go(mid_copy(a, k, i - 2))
        if 0 <= t - 1 < len(units):
            a, k = units[t - 1]
            for i in (1, 0):
                mid_copy(a, k, i).wait_recv()
                add(mid.at[a, k, i], near.at[a, k, i])
                if i:
                    go(far_copy(a, k))
        if 0 <= t - 2 < len(units):
            a, k = units[t - 2]
            far_copy(a, k).wait_recv()
            add(far.at[a, k], mid.at[a, k, 0])
            if k:
                go(line_copy(a, k, lax.rem(m + k, mp)))
    for a in range(BLOCKS):
        total = far[a, 0].astype(F32)
        for k in range(1, mp):
            remote(line.at[a, k], line.at[a, k], send.at[a, k, 7], recv.at[a, k, 7], (d, m)).wait_recv()
            total = total + line[a, k].astype(F32)
        out_ref[a, s] = total.astype(BF16)
        go(spread(a, 0, s, first))
        go(spread(a, 1, s, second))
        go(spread(a, 3, s, 1))
    for a in range(BLOCKS):
        spread(a, 0, s1, first).wait_recv()
        go(spread(a, 2, s1, second))
        go(spread(a, 4, s1, 1))
        spread(a, 1, s2, second).wait_recv()
        go(spread(a, 5, s2, 1))
    for a in range(BLOCKS):
        spread(a, 2, s3, second).wait_recv()
        go(spread(a, 6, s3, 1))
    for a in range(BLOCKS):
        for i, piece in ((3, s), (4, s1), (5, s2), (6, s3)):
            spread(a, i, flip(piece, 1), 1).wait_recv()
    for copy in sent:
        copy.wait_send()


def reduce_grads(grads, mp):
    blocks, _, inner, rows, width = grads.shape
    return pl.pallas_call(
        partial(reduce_kernel, mp),
        out_shape=jax.ShapeDtypeStruct((blocks, inner, rows, width), BF16),
        in_specs=[pl.BlockSpec(memory_space=pltpu.VMEM)],
        out_specs=pl.BlockSpec(memory_space=pltpu.VMEM),
        scratch_shapes=[
            pltpu.VMEM((blocks, mp, 4, rows, width), BF16),
            pltpu.VMEM((blocks, mp, 2, rows, width), BF16),
            pltpu.VMEM((blocks, mp, rows, width), BF16),
            pltpu.VMEM((blocks, mp, rows, width), BF16),
            pltpu.SemaphoreType.DMA((blocks, mp + 1, 8)),
            pltpu.SemaphoreType.DMA((blocks, mp + 1, 8)),
        ],
        input_output_aliases={},
        compiler_params=pltpu.CompilerParams(
            collective_id=1, has_side_effects=True, vmem_limit_bytes=63 * 1024 * 1024
        ),
    )(grads)


def norm_rows(hidden, gain_vec, shift_vec):
    row_mean = jnp.mean(hidden, axis=-1, keepdims=True)
    centred = hidden - row_mean
    variance = jnp.mean(centred * centred, axis=-1, keepdims=True)
    row_scale = lax.rsqrt(variance + EPS)
    normed = centred * row_scale
    return (normed * gain_vec + shift_vec, normed, row_scale)


def norm_back(grad_out, normed, row_scale, gain_vec):
    grad_normed = grad_out * gain_vec
    inner_mean = jnp.mean(grad_normed, axis=-1, keepdims=True)
    cross_mean = jnp.mean(grad_normed * normed, axis=-1, keepdims=True)
    grad_in = row_scale * (grad_normed - inner_mean - normed * cross_mean)
    return (grad_in, jnp.sum(grad_out * normed, axis=0), jnp.sum(grad_out, axis=0))


def on_device(
    token_block,
    token_offset,
    lengths,
    group_counts,
    table,
    weight_qkv,
    bias_query,
    bias_value,
    weight_out,
    bias_out,
    gain_one,
    shift_one,
    weight_in,
    bias_in,
    weight_down,
    bias_down,
    gain_two,
    shift_two,
    cotangent,
):
    axes = ("dp", "mp")
    devices = lax.axis_size(axes)
    mp = lax.axis_size("mp")
    dp = lax.axis_size("dp")
    me = lax.axis_index(axes)
    tok_rows = token_offset.shape[0]
    width = table.shape[1]
    sent_local = lengths.shape[0]
    shard_rows = weight_down.shape[0]
    qkv_rows = weight_qkv.shape[1]
    own_heads = qkv_rows // (3 * HD)
    heads = own_heads * mp
    slice_rows = shard_rows // INNER

    own = jnp.stack([jnp.concatenate([weight_qkv.T, weight_out], axis=0), weight_in, weight_down])
    whole = gather_weights(own.reshape(BLOCKS, INNER, slice_rows, width), mp)
    whole = whole.reshape(BLOCKS, mp, shard_rows, width)
    qkv_t = whole[0, :, :qkv_rows].reshape(heads * 3 * HD, width)
    w_out = whole[0, :, qkv_rows:].reshape(heads * HD, width)
    w_in = whole[1]
    w_down = whole[2]
    bias_all = lax.all_gather(jnp.concatenate([bias_query, bias_value, bias_in]), "mp", axis=0, tiled=False)
    b_query = bias_all[:, : own_heads * HD].reshape(heads, HD).astype(F32)
    b_value = bias_all[:, own_heads * HD : 2 * own_heads * HD].reshape(heads, HD).astype(F32)
    b_in = bias_all[:, 2 * own_heads * HD :].astype(F32)

    capacity = max(2, 2 * tok_rows // devices)
    token_owner = token_block[:, 0]
    owner_hits = (token_owner[:, None] == jnp.arange(devices, dtype=jnp.int32)[None, :]).astype(jnp.int32)
    slot_index = jnp.sum((jnp.cumsum(owner_hits, axis=0) - 1) * owner_hits, axis=1)
    slot_place = token_owner * capacity + slot_index
    requests = jnp.full((devices * capacity,), -1, jnp.int32).at[slot_place].set(token_offset)
    wanted = lax.all_to_all(requests.reshape(devices, capacity), axes, split_axis=0, concat_axis=0, tiled=True)
    slot_live = wanted >= 0
    wanted_rows = jnp.maximum(wanted, 0)
    fetched = lax.all_to_all(table[wanted_rows], axes, split_axis=0, concat_axis=0, tiled=True)
    embedded = fetched.reshape(devices * capacity, width)[slot_place]

    total_sent = sent_local * devices
    group_num = group_counts.shape[0]
    sent_index = me * sent_local + jnp.arange(sent_local, dtype=jnp.int32)
    offsets = jnp.cumsum(group_counts) - group_counts
    member = (sent_index[:, None] >= offsets[None, :]) & (sent_index[:, None] < (offsets + group_counts)[None, :])
    group_weight = total_sent / (group_num * group_counts.astype(F32))
    sent_weight = jnp.sum(jnp.where(member, group_weight[None, :], F32(0.0)), axis=1)
    positions = jnp.arange(SEQ, dtype=jnp.int32)
    token_live = (positions[None, :] < lengths[:, None]).astype(F32)
    row_weight = (token_live * sent_weight[:, None]).reshape(tok_rows)
    count_local = jnp.sum(lengths).astype(F32)

    dot = partial(jnp.einsum, preferred_element_type=F32)
    mixed = dot("td,cd->tc", embedded, qkv_t).reshape(sent_local, SEQ, heads, 3, HD)
    queries = (mixed[:, :, :, 0] + b_query).astype(BF16)
    key_rows = mixed[:, :, :, 1].astype(BF16)
    value_rows = (mixed[:, :, :, 2] + b_value).astype(BF16)
    scores = dot("sqhe,skhe->shqk", queries, key_rows) * 0.125
    valid = positions[None, :] < lengths[:, None]
    scores = jnp.where(valid[:, None, None, :], scores, F32(-1e30))
    probs = jax.nn.softmax(scores, axis=-1)
    probs_low = probs.astype(BF16)
    context = dot("shqk,skhe->sqhe", probs_low, value_rows).astype(BF16)
    context_rows = context.reshape(tok_rows, heads * HD)
    gain_one_f = gain_one.astype(F32)
    gain_two_f = gain_two.astype(F32)
    first_out, normed_one, scale_one = norm_rows(
        embedded.astype(F32) + dot("tc,cd->td", context_rows, w_out) + bias_out.astype(F32),
        gain_one_f,
        shift_one.astype(F32),
    )
    first_low = first_out.astype(BF16)
    hidden_pre = dot("td,mdf->tmf", first_low, w_in) + b_in
    gelu_val, gelu_pull = jax.vjp(partial(jax.nn.gelu, approximate=False), hidden_pre)
    hidden_act = gelu_val.astype(BF16)
    down_sum = dot("tmf,mfd->td", hidden_act, w_down)
    final_out, normed_two, scale_two = norm_rows(
        first_out + down_sum + bias_down.astype(F32), gain_two_f, shift_two.astype(F32)
    )
    activations = final_out.astype(BF16)
    grad_final = row_weight[:, None] * cotangent.astype(F32)
    grad_h2, grad_gain_two, grad_shift_two = norm_back(grad_final, normed_two, scale_two, gain_two_f)
    grad_bias_down = jnp.sum(grad_h2, axis=0)
    grad_down = grad_h2.astype(BF16)
    grad_w_down = dot("tmf,td->mfd", hidden_act, grad_down)
    grad_act = dot("td,mfd->tmf", grad_down, w_down)
    grad_pre = gelu_pull(grad_act)[0].astype(BF16)
    grad_bias_in = jnp.sum(grad_pre.astype(F32), axis=0)
    grad_w_in = dot("td,tmf->mdf", first_low, grad_pre)
    grad_first = grad_h2 + dot("tmf,mdf->td", grad_pre, w_in)
    grad_h1, grad_gain_one, grad_shift_one = norm_back(grad_first, normed_one, scale_one, gain_one_f)
    grad_bias_out = jnp.sum(grad_h1, axis=0)
    grad_attn = grad_h1.astype(BF16)
    grad_w_out = dot("tc,td->cd", context_rows, grad_attn)
    grad_context = dot("td,cd->tc", grad_attn, w_out).astype(BF16).reshape(sent_local, SEQ, heads, HD)
    grad_probs = dot("sqhe,skhe->shqk", grad_context, value_rows)
    grad_value = dot("shqk,sqhe->skhe", probs_low, grad_context).astype(BF16)
    grad_scores = (probs * (grad_probs - jnp.sum(grad_probs * probs, axis=-1, keepdims=True))).astype(BF16)
    grad_query = (dot("shqk,skhe->sqhe", grad_scores, key_rows) * 0.125).astype(BF16)
    grad_key = (dot("shqk,sqhe->skhe", grad_scores, queries) * 0.125).astype(BF16)
    grad_mixed = jnp.stack([grad_query, grad_key, grad_value], axis=3).reshape(tok_rows, heads * 3 * HD)
    grad_w_qkv = dot("tc,td->cd", grad_mixed, embedded)
    grad_bias_query = jnp.sum(grad_query.astype(F32), axis=(0, 1)).reshape(mp, own_heads * HD)
    grad_bias_value = jnp.sum(grad_value.astype(F32), axis=(0, 1)).reshape(mp, own_heads * HD)
    grad_embed = grad_h1 + dot("tc,cd->td", grad_mixed, qkv_t)

    grads = jnp.stack(
        [
            jnp.concatenate(
                [grad_w_qkv.reshape(mp, qkv_rows, width), grad_w_out.reshape(mp, own_heads * HD, width)], axis=1
            ),
            grad_w_in,
            grad_w_down,
        ]
    ).astype(BF16)
    summed = reduce_grads(grads.reshape(BLOCKS, mp, INNER, slice_rows, width), mp)
    group = summed
    for step in range(1, dp // INNER):
        shift = [(i, (i + step * INNER) % dp) for i in range(dp)]
        summed = (summed.astype(F32) + lax.ppermute(group, "dp", shift).astype(F32)).astype(BF16)
    summed = summed.reshape(BLOCKS, shard_rows, width)

    small = lax.psum(
        (
            count_local,
            grad_gain_one,
            grad_shift_one,
            grad_bias_out,
            grad_gain_two,
            grad_shift_two,
            grad_bias_down,
            grad_bias_query,
            grad_bias_value,
            grad_bias_in,
        ),
        axes,
    )
    factor = lax.rsqrt(small[0])
    gain_one_s, shift_one_s, bias_out_s, gain_two_s, shift_two_s, bias_down_s = (v * factor for v in small[1:7])
    m = lax.axis_index("mp")
    bias_query_s, bias_value_s, bias_in_s = (v[m] * factor for v in small[7:])

    outgoing = jnp.zeros((devices * capacity, width), BF16).at[slot_place].set(grad_embed.astype(BF16))
    incoming = lax.all_to_all(
        outgoing.reshape(devices, capacity, width), axes, split_axis=0, concat_axis=0, tiled=True
    )
    received = jnp.where(slot_live[..., None], incoming.astype(F32), F32(0.0)).reshape(devices * capacity, width)
    grad_table = jnp.zeros(table.shape, F32).at[wanted_rows.reshape(-1)].add(received * factor)
    scaled = summed.astype(F32) * factor
    return (
        activations,
        grad_table,
        scaled[0, :qkv_rows].T,
        bias_query_s,
        bias_value_s,
        scaled[0, qkv_rows:],
        bias_out_s,
        gain_one_s,
        shift_one_s,
        scaled[1],
        bias_in_s,
        scaled[2],
        bias_down_s,
        gain_two_s,
        shift_two_s,
    )


def solution(mesh):
    placed = (
        P(("dp", "mp"), None),
        P(("dp", "mp")),
        P(("dp", "mp")),
        P(),
        P(("dp", "mp"), None),
        P(None, "mp"),
        P("mp"),
        P("mp"),
        P("mp", None),
        P(),
        P(),
        P(),
        P(None, "mp"),
        P("mp"),
        P("mp", None),
        P(),
        P(),
        P(),
        P(("dp", "mp"), None),
    )
    return jax.shard_map(
        on_device,
        mesh=mesh,
        in_specs=placed,
        out_specs=(
            P(("dp", "mp"), None),
            P(("dp", "mp"), None),
            P(None, "mp"),
            P("mp"),
            P("mp"),
            P("mp", None),
            P(),
            P(),
            P(),
            P(None, "mp"),
            P("mp"),
            P("mp", None),
            P(),
            P(),
            P(),
        ),
        check_vma=False,
    )
```

```python
from functools import partial

import jax
import jax.numpy as jnp
from jax import lax
from jax.experimental import pallas as pl
from jax.experimental.pallas import tpu as pltpu
from jax.sharding import PartitionSpec as P

HD = 64
SEQ = 64
EPS = 1e-12
MESH = pl.DeviceIdType.MESH
F32 = jnp.float32
BF16 = jnp.bfloat16

INNER = 8
BLOCKS = 3


def position():
    d = lax.axis_index("dp")
    m = lax.axis_index("mp")
    core = lax.rem(d, 2)
    first = 4 - 2 * core
    second = 2 + 2 * core
    return d, m, first, second


def flip(d, bit):
    return d + bit - 2 * bit * lax.rem(lax.div(d, bit), 2)


def place(a, owner, piece, mp):
    if a == 0:
        return lax.div(piece, 2) * (2 * mp) + owner * 2 + lax.rem(piece, 2)
    return owner * INNER + piece


def nearest(m, mp):
    table = []
    for at in range(mp):
        owners = sorted((abs(o - at), o < at, (o - at) % mp) for o in range(mp) if o != at)
        table.append([entry[2] for entry in owners])
    offsets = []
    for i in range(mp - 1):
        k = table[0][i]
        for at in range(1, mp):
            k = jnp.where(m == at, table[at][i], k)
        offsets.append(k)
    return offsets


def enter_all(me, mp, devices):
    barrier = pltpu.get_barrier_semaphore()

    def greet(j, _):
        peer = lax.rem(me + j, devices)
        pl.semaphore_signal(
            barrier, inc=1, device_id=(lax.div(peer, mp), lax.rem(peer, mp)), device_id_type=MESH
        )
        return 0

    lax.fori_loop(1, devices, greet, 0)
    pl.semaphore_wait(barrier, devices - 1)


def remote(src, dst, send, recv, peer):
    return pltpu.make_async_remote_copy(
        src_ref=src, dst_ref=dst, send_sem=send, recv_sem=recv, device_id=peer, device_id_type=MESH
    )


def row_exchange(me, mp, devices, rows_ref, rows_out, send, recv, own_sem):
    def copy_to(j):
        peer = lax.rem(me + j, devices)
        return remote(
            rows_ref.at[peer], rows_out.at[me], send.at[j], recv.at[j], (lax.div(peer, mp), lax.rem(peer, mp))
        )

    def start():
        pltpu.make_async_copy(rows_ref.at[me], rows_out.at[me], own_sem).start()

        def body(j, _):
            copy_to(j).start()
            return 0

        lax.fori_loop(1, devices, body, 0)

    def finish():
        pltpu.make_async_copy(rows_ref.at[me], rows_out.at[me], own_sem).wait()

        def body(j, _):
            peer = lax.rem(me + devices - j, devices)
            back = remote(
                rows_ref.at[peer], rows_out.at[peer], send.at[j], recv.at[j], (lax.div(peer, mp), lax.rem(peer, mp))
            )
            back.wait_recv()
            back.wait_send()
            return 0

        lax.fori_loop(1, devices, body, 0)

    return start, finish


def gather_kernel(
    mp, devices, own_ref, bias_ref, rows_ref, out_ref, bias_out, rows_out, send, recv, z_send, own_sem, b_send, b_recv, r_send, r_recv
):
    d, m, first, second = position()
    me = d * mp + m
    enter_all(me, mp, devices)
    s = lax.rem(d, INNER)
    s1 = flip(s, first)
    s2 = flip(s, second)
    s3 = flip(s1, second)
    above = jnp.minimum(m + 1, mp - 1)
    below = jnp.maximum(m - 1, 0)

    def z_copy(a, owner, to, slot):
        at = out_ref.at[a, place(a, owner, s, mp)]
        k = lax.rem(owner - to + mp, mp)
        return remote(at, at, z_send.at[a, slot], recv.at[a, k, 0], (d, to))

    def own_z(a, to, slot):
        at = out_ref.at[a, place(a, m, s, mp)]
        k = lax.rem(m - to + mp, mp)
        return remote(own_ref.at[a, s], at, z_send.at[a, slot], recv.at[a, k, 0], (d, to))

    def start_own(a):
        @pl.when(m < mp - 1)
        def _():
            own_z(a, above, 0).start()

        @pl.when(m > 0)
        def _():
            own_z(a, below, 1).start()

    def own_copy(a, piece):
        return pltpu.make_async_copy(own_ref.at[a, piece], out_ref.at[a, place(a, m, piece, mp)], own_sem.at[a, piece])

    def bias_copy(k):
        return remote(bias_ref, bias_out.at[m], b_send.at[k], b_recv.at[mp - k], (d, lax.rem(m + k, mp)))

    start_rows, finish_rows = row_exchange(me, mp, devices, rows_ref, rows_out, r_send, r_recv, own_sem.at[BLOCKS, 0])
    for k in range(1, mp):
        bias_copy(k).start()
    bias_own = pltpu.make_async_copy(bias_ref, bias_out.at[m], own_sem.at[BLOCKS, 1])
    bias_own.start()
    start_own(0)
    start_rows()
    for a in range(1, BLOCKS):
        start_own(a)
    for a in range(BLOCKS):
        for piece in range(INNER):
            own_copy(a, piece).start()

    def hop(a, k, piece, slot, bit):
        ref = out_ref.at[a, place(a, lax.rem(m + k, mp), piece, mp)]
        return remote(ref, ref, send.at[a, k, slot], recv.at[a, k, slot], (flip(d, bit), m))

    offsets = nearest(m, mp)
    units = [(a, i) for a in range(BLOCKS) for i in range(mp - 1)]
    sent = []

    def go(copy):
        copy.start()
        sent.append(copy)

    def z_forward(a, i):
        owner = lax.rem(m + offsets[i], mp)
        return owner, z_copy(a, owner, below, 2 + i), z_copy(a, owner, above, 2 + i)

    for t in range(len(units) + 3):
        if t < len(units):
            a, i = units[t]
            k = offsets[i]
            owner, down, up = z_forward(a, i)
            remote(own_ref.at[a, s], out_ref.at[a, place(a, owner, s, mp)], send.at[a, k, 0], recv.at[a, k, 0], (d, owner)).wait_recv()

            @pl.when(jnp.logical_and(owner > m, m > 0))
            def _():
                down.start()

            @pl.when(jnp.logical_and(owner < m, m < mp - 1))
            def _():
                up.start()

            go(hop(a, k, s, 1, first))
            go(hop(a, k, s, 2, second))
            go(hop(a, k, s, 4, 1))
        if 0 <= t - 1 < len(units):
            a, i = units[t - 1]
            k = offsets[i]
            hop(a, k, s1, 1, first).wait_recv()
            go(hop(a, k, s1, 3, second))
            go(hop(a, k, s1, 5, 1))
        if 0 <= t - 2 < len(units):
            a, i = units[t - 2]
            k = offsets[i]
            hop(a, k, s2, 2, second).wait_recv()
            go(hop(a, k, s2, 6, 1))
            hop(a, k, s3, 3, second).wait_recv()
            go(hop(a, k, s3, 7, 1))
        if 0 <= t - 3 < len(units):
            a, i = units[t - 3]
            k = offsets[i]
            for slot, piece in ((4, s), (5, s1), (6, s2), (7, s3)):
                hop(a, k, flip(piece, 1), slot, 1).wait_recv()
    finish_rows()
    for k in range(1, mp):
        remote(bias_ref, bias_out.at[lax.rem(m + k, mp)], b_send.at[k], b_recv.at[k], (d, lax.rem(m + k, mp))).wait_recv()
        bias_copy(k).wait_send()
    bias_own.wait()
    for copy in sent:
        copy.wait_send()
    for a in range(BLOCKS):
        for piece in range(INNER):
            own_copy(a, piece).wait()

        @pl.when(m < mp - 1)
        def _():
            own_z(a, above, 0).wait_send()

        @pl.when(m > 0)
        def _():
            own_z(a, below, 1).wait_send()

        for i in range(mp - 1):
            owner, down, up = z_forward(a, i)

            @pl.when(jnp.logical_and(owner > m, m > 0))
            def _():
                down.wait_send()

            @pl.when(jnp.logical_and(owner < m, m < mp - 1))
            def _():
                up.wait_send()


def gather_weights(own, bias, rows, mp):
    _, inner, piece_rows, width = own.shape
    devices = rows.shape[0]
    vmem = pl.BlockSpec(memory_space=pltpu.VMEM)
    dma = pltpu.SemaphoreType.DMA
    return pl.pallas_call(
        partial(gather_kernel, mp, devices),
        out_shape=(
            jax.ShapeDtypeStruct((BLOCKS, mp * inner, piece_rows, width), BF16),
            jax.ShapeDtypeStruct((mp, *bias.shape), BF16),
            jax.ShapeDtypeStruct(rows.shape, BF16),
        ),
        in_specs=[vmem] * 3,
        out_specs=(vmem,) * 3,
        scratch_shapes=[
            dma((BLOCKS, mp, 8)),
            dma((BLOCKS, mp, 8)),
            dma((BLOCKS, 1 + mp)),
            dma((BLOCKS + 1, INNER)),
            dma((mp,)),
            dma((mp,)),
            dma((devices,)),
            dma((devices,)),
        ],
        compiler_params=pltpu.CompilerParams(
            collective_id=0, has_side_effects=True, vmem_limit_bytes=60 * 1024 * 1024
        ),
    )(own, bias, rows)


def reduce_kernel(
    mp,
    devices,
    grad_ref,
    small_ref,
    rows_ref,
    out_ref,
    small_out,
    rows_out,
    near,
    mid,
    far,
    line,
    part,
    part_in,
    send,
    recv,
    p_send,
    p_recv,
    r_send,
    r_recv,
    own_sem,
):
    d, m, first, second = position()
    me = d * mp + m
    enter_all(me, mp, devices)
    s = lax.rem(d, INNER)
    s1 = flip(s, first)
    s2 = flip(s, second)
    s3 = flip(s1, second)
    mine = (s, s1, s2, s3)
    other = tuple(flip(piece, 1) for piece in (s, s2, s1, s3))
    sent = []

    def go(copy):
        copy.start()
        sent.append(copy)

    units = [(a, k) for a in range(BLOCKS) for k in (*range(1, mp), 0)]

    def add(into, more):
        into[...] = (into[...].astype(F32) + more[...].astype(F32)).astype(BF16)

    def near_copy(a, k, i, owner):
        return remote(
            grad_ref.at[a, place(a, owner, other[i], mp)], near.at[a, k, i], send.at[a, k, i], recv.at[a, k, i], (flip(d, 1), m)
        )

    def mid_copy(a, k, i):
        return remote(
            near.at[a, k, 2 + i], mid.at[a, k, i], send.at[a, k, 4 + i], recv.at[a, k, 4 + i], (flip(d, second), m)
        )

    def far_copy(a, k):
        return remote(mid.at[a, k, 1], far.at[a, k], send.at[a, k, 6], recv.at[a, k, 6], (flip(d, first), m))

    def line_copy(a, k, owner):
        return remote(far.at[a, k], line.at[a, mp - k], send.at[a, k, 7], recv.at[a, mp - k, 7], (d, owner))

    def spread(a, i, piece, bit):
        ref = out_ref.at[a, piece]
        return remote(ref, ref, send.at[a, mp, i], recv.at[a, mp, i], (flip(d, bit), m))

    def part_copy(i):
        source = small_ref if i == 0 else part.at[i - 1]
        return remote(source, part_in.at[i], p_send.at[i], p_recv.at[i], (flip(d, 2**i), m))

    def total_copy(k):
        return remote(
            part.at[2], part_in.at[3 + m], p_send.at[2 + k], p_recv.at[3 + m], (d, lax.rem(m + k, mp))
        )

    def part_step(i):
        part_copy(i).wait_recv()
        part[i] = (small_ref[...] if i == 0 else part[i - 1]) + part_in[i]
        if i < 2:
            go(part_copy(i + 1))
        else:
            for k in range(1, mp):
                go(total_copy(k))

    start_rows, finish_rows = row_exchange(me, mp, devices, rows_ref, rows_out, r_send, r_recv, own_sem.at[0])
    go(part_copy(0))
    for n, (a, k) in enumerate(units):
        for i in (2, 3, 0, 1):
            go(near_copy(a, k, i, lax.rem(m + k, mp)))
        if n == 0:
            start_rows()
    for t in range(len(units) + 2):
        if t < len(units):
            a, k = units[t]
            owner = lax.rem(m + k, mp)
            for i in (2, 3, 0, 1):
                near_copy(a, k, i, owner).wait_recv()
                add(near.at[a, k, i], grad_ref.at[a, place(a, owner, mine[i], mp)])
                if i >= 2:
                    go(mid_copy(a, k, i - 2))
        if 0 <= t - 1 < len(units):
            a, k = units[t - 1]
            for i in (1, 0):
                mid_copy(a, k, i).wait_recv()
                add(mid.at[a, k, i], near.at[a, k, i])
                if i:
                    go(far_copy(a, k))
        if 0 <= t - 2 < len(units):
            a, k = units[t - 2]
            far_copy(a, k).wait_recv()
            add(far.at[a, k], mid.at[a, k, 0])
            if k:
                go(line_copy(a, k, lax.rem(m + k, mp)))
        if t in (2, 5, 8):
            part_step(t // 3)
    for a in range(BLOCKS):
        total = far[a, 0].astype(F32)
        for k in range(1, mp):
            remote(line.at[a, k], line.at[a, k], send.at[a, k, 7], recv.at[a, k, 7], (d, m)).wait_recv()
            total = total + line[a, k].astype(F32)
        out_ref[a, s] = total.astype(BF16)
        go(spread(a, 0, s, first))
        go(spread(a, 1, s, second))
        go(spread(a, 3, s, 1))
    for a in range(BLOCKS):
        spread(a, 0, s1, first).wait_recv()
        go(spread(a, 2, s1, second))
        go(spread(a, 4, s1, 1))
        spread(a, 1, s2, second).wait_recv()
        go(spread(a, 5, s2, 1))
    part_in[3 + m] = part[2]
    for k in range(1, mp):
        owner = lax.rem(m + k, mp)
        remote(part.at[2], part_in.at[3 + owner], p_send.at[2 + k], p_recv.at[3 + owner], (d, owner)).wait_recv()
    whole_sum = part_in[3]
    for k in range(1, mp):
        whole_sum = whole_sum + part_in[3 + k]
    small_out[...] = whole_sum
    for a in range(BLOCKS):
        spread(a, 2, s3, second).wait_recv()
        go(spread(a, 6, s3, 1))
    finish_rows()
    for a in range(BLOCKS):
        for i, piece in ((3, s), (4, s1), (5, s2), (6, s3)):
            spread(a, i, flip(piece, 1), 1).wait_recv()
    for copy in sent:
        copy.wait_send()


def reduce_grads(grads, small, rows, mp):
    blocks, pieces, piece_rows, width = grads.shape
    devices = rows.shape[0]
    vmem = pl.BlockSpec(memory_space=pltpu.VMEM)
    dma = pltpu.SemaphoreType.DMA
    return pl.pallas_call(
        partial(reduce_kernel, mp, devices),
        out_shape=(
            jax.ShapeDtypeStruct((blocks, pieces // mp, piece_rows, width), BF16),
            jax.ShapeDtypeStruct(small.shape, F32),
            jax.ShapeDtypeStruct(rows.shape, BF16),
        ),
        in_specs=[vmem] * 3,
        out_specs=(vmem,) * 3,
        scratch_shapes=[
            pltpu.VMEM((blocks, mp, 4, piece_rows, width), BF16),
            pltpu.VMEM((blocks, mp, 2, piece_rows, width), BF16),
            pltpu.VMEM((blocks, mp, piece_rows, width), BF16),
            pltpu.VMEM((blocks, mp, piece_rows, width), BF16),
            pltpu.VMEM((3, *small.shape), F32),
            pltpu.VMEM((3 + mp, *small.shape), F32),
            dma((blocks, mp + 1, 8)),
            dma((blocks, mp + 1, 8)),
            dma((2 + mp,)),
            dma((3 + mp,)),
            dma((devices,)),
            dma((devices,)),
            dma((1,)),
        ],
        compiler_params=pltpu.CompilerParams(
            collective_id=1, has_side_effects=True, vmem_limit_bytes=63 * 1024 * 1024
        ),
    )(grads, small, rows)


def norm_rows(hidden, gain_vec, shift_vec):
    row_mean = jnp.mean(hidden, axis=-1, keepdims=True)
    centred = hidden - row_mean
    variance = jnp.mean(centred * centred, axis=-1, keepdims=True)
    row_scale = lax.rsqrt(variance + EPS)
    normed = centred * row_scale
    return (normed * gain_vec + shift_vec, normed, row_scale)


def norm_back(grad_out, normed, row_scale, gain_vec):
    grad_normed = grad_out * gain_vec
    inner_mean = jnp.mean(grad_normed, axis=-1, keepdims=True)
    cross_mean = jnp.mean(grad_normed * normed, axis=-1, keepdims=True)
    grad_in = row_scale * (grad_normed - inner_mean - normed * cross_mean)
    return (grad_in, jnp.sum(grad_out * normed, axis=0), jnp.sum(grad_out, axis=0))


def on_device(
    token_block,
    token_offset,
    lengths,
    group_counts,
    table,
    weight_qkv,
    bias_query,
    bias_value,
    weight_out,
    bias_out,
    gain_one,
    shift_one,
    weight_in,
    bias_in,
    weight_down,
    bias_down,
    gain_two,
    shift_two,
    cotangent,
):
    axes = ("dp", "mp")
    devices = lax.axis_size(axes)
    mp = lax.axis_size("mp")
    dp = lax.axis_size("dp")
    me = lax.axis_index(axes)
    tok_rows = token_offset.shape[0]
    width = table.shape[1]
    sent_local = lengths.shape[0]
    shard_rows = weight_down.shape[0]
    qkv_rows = weight_qkv.shape[1]
    own_heads = qkv_rows // (3 * HD)
    heads = own_heads * mp
    slice_rows = shard_rows // INNER

    kinds = weight_qkv.reshape(width, own_heads, 3, HD).transpose(2, 1, 3, 0).reshape(qkv_rows, width)
    own = jnp.stack([jnp.concatenate([kinds, weight_out], axis=0), weight_in, weight_down])
    bias_own = jnp.concatenate([bias_query, bias_value, bias_in])
    bias_rows = bias_own.shape[0] // 128
    bias_own = jnp.pad(bias_own.reshape(bias_rows, 128), ((0, -bias_rows % 16), (0, 0)))

    capacity = max(2, 2 * tok_rows // devices)
    token_owner = token_block[:, 0]
    owner_hits = (token_owner[:, None] == jnp.arange(devices, dtype=jnp.int32)[None, :]).astype(jnp.int32)
    slot_index = jnp.sum((jnp.cumsum(owner_hits, axis=0) - 1) * owner_hits, axis=1)
    slot_place = token_owner * capacity + slot_index
    requests = jnp.full((devices * capacity,), -1, jnp.int32).at[slot_place].set(token_offset)
    wanted = lax.all_to_all(requests.reshape(devices, capacity), axes, split_axis=0, concat_axis=0, tiled=True)
    slot_live = wanted >= 0
    wanted_rows = jnp.maximum(wanted, 0)
    whole, bias_all, fetched = gather_weights(
        own.reshape(BLOCKS, INNER, slice_rows, width), bias_own, table[wanted_rows], mp
    )
    embedded = fetched.reshape(devices * capacity, width)[slot_place]
    w_query, w_key, w_value, w_out = whole[0].reshape(4, heads * HD, width)
    w_in = whole[1].reshape(mp, shard_rows, width)
    w_down = whole[2].reshape(mp, shard_rows, width)
    bias_all = bias_all.reshape(mp, -1)
    b_query = bias_all[:, : own_heads * HD].reshape(heads, HD).astype(F32)
    b_value = bias_all[:, own_heads * HD : 2 * own_heads * HD].reshape(heads, HD).astype(F32)
    b_in = bias_all[:, 2 * own_heads * HD : 2 * own_heads * HD + bias_in.shape[0]].astype(F32)

    total_sent = sent_local * devices
    group_num = group_counts.shape[0]
    sent_index = me * sent_local + jnp.arange(sent_local, dtype=jnp.int32)
    offsets = jnp.cumsum(group_counts) - group_counts
    member = (sent_index[:, None] >= offsets[None, :]) & (sent_index[:, None] < (offsets + group_counts)[None, :])
    group_weight = total_sent / (group_num * group_counts.astype(F32))
    sent_weight = jnp.sum(jnp.where(member, group_weight[None, :], F32(0.0)), axis=1)
    positions = jnp.arange(SEQ, dtype=jnp.int32)
    token_live = (positions[None, :] < lengths[:, None]).astype(F32)
    row_weight = (token_live * sent_weight[:, None]).reshape(tok_rows)
    count_local = jnp.sum(lengths).astype(F32)

    dot = partial(jnp.einsum, preferred_element_type=F32)
    by_head = (sent_local, SEQ, heads, HD)
    queries = (dot("td,cd->tc", embedded, w_query).reshape(by_head) + b_query).astype(BF16)
    key_rows = dot("td,cd->tc", embedded, w_key).reshape(by_head).astype(BF16)
    value_rows = (dot("td,cd->tc", embedded, w_value).reshape(by_head) + b_value).astype(BF16)
    scores = dot("sqhe,skhe->shqk", queries, key_rows) * 0.125
    valid = positions[None, :] < lengths[:, None]
    scores = jnp.where(valid[:, None, None, :], scores, F32(-1e30))
    probs = jax.nn.softmax(scores, axis=-1)
    probs_low = probs.astype(BF16)
    context = dot("shqk,skhe->sqhe", probs_low, value_rows).astype(BF16)
    context_rows = context.reshape(tok_rows, heads * HD)
    gain_one_f = gain_one.astype(F32)
    gain_two_f = gain_two.astype(F32)
    first_out, normed_one, scale_one = norm_rows(
        embedded.astype(F32) + dot("tc,cd->td", context_rows, w_out) + bias_out.astype(F32),
        gain_one_f,
        shift_one.astype(F32),
    )
    first_low = first_out.astype(BF16)
    hidden_pre = dot("td,mdf->tmf", first_low, w_in) + b_in
    gelu_val, gelu_pull = jax.vjp(partial(jax.nn.gelu, approximate=False), hidden_pre)
    hidden_act = gelu_val.astype(BF16)
    down_sum = dot("tmf,mfd->td", hidden_act, w_down)
    final_out, normed_two, scale_two = norm_rows(
        first_out + down_sum + bias_down.astype(F32), gain_two_f, shift_two.astype(F32)
    )
    activations = final_out.astype(BF16)
    grad_final = row_weight[:, None] * cotangent.astype(F32)
    grad_h2, grad_gain_two, grad_shift_two = norm_back(grad_final, normed_two, scale_two, gain_two_f)
    grad_bias_down = jnp.sum(grad_h2, axis=0)
    grad_down = grad_h2.astype(BF16)
    grad_w_down = dot("tmf,td->mfd", hidden_act, grad_down)
    grad_act = dot("td,mfd->tmf", grad_down, w_down)
    grad_pre = gelu_pull(grad_act)[0].astype(BF16)
    grad_bias_in = jnp.sum(grad_pre.astype(F32), axis=0)
    grad_w_in = dot("td,tmf->mdf", first_low, grad_pre)
    grad_first = grad_h2 + dot("tmf,mdf->td", grad_pre, w_in)
    grad_h1, grad_gain_one, grad_shift_one = norm_back(grad_first, normed_one, scale_one, gain_one_f)
    grad_bias_out = jnp.sum(grad_h1, axis=0)
    grad_attn = grad_h1.astype(BF16)
    grad_w_out = dot("tc,td->cd", context_rows, grad_attn)
    grad_context = dot("td,cd->tc", grad_attn, w_out).astype(BF16).reshape(sent_local, SEQ, heads, HD)
    grad_probs = dot("sqhe,skhe->shqk", grad_context, value_rows)
    grad_value = dot("shqk,sqhe->skhe", probs_low, grad_context).astype(BF16)
    grad_scores = (probs * (grad_probs - jnp.sum(grad_probs * probs, axis=-1, keepdims=True))).astype(BF16)
    grad_query = (dot("shqk,skhe->sqhe", grad_scores, key_rows) * 0.125).astype(BF16)
    grad_key = (dot("shqk,sqhe->skhe", grad_scores, queries) * 0.125).astype(BF16)
    flat = (tok_rows, heads * HD)
    grad_query, grad_key, grad_value = grad_query.reshape(flat), grad_key.reshape(flat), grad_value.reshape(flat)
    grad_bias_query = jnp.sum(grad_query.astype(F32), axis=0)
    grad_bias_value = jnp.sum(grad_value.astype(F32), axis=0)
    grad_embed = (
        grad_h1
        + dot("tc,cd->td", grad_query, w_query)
        + dot("tc,cd->td", grad_key, w_key)
        + dot("tc,cd->td", grad_value, w_value)
    )
    kinds = [dot("tc,td->cd", part, embedded) for part in (grad_query, grad_key, grad_value)]
    grads = jnp.stack(
        [
            jnp.stack([*kinds, grad_w_out]).reshape(mp * INNER, slice_rows, width),
            grad_w_in.reshape(mp * INNER, slice_rows, width),
            grad_w_down.reshape(mp * INNER, slice_rows, width),
        ]
    ).astype(BF16)
    vectors = [grad_gain_one, grad_shift_one, grad_bias_out, grad_gain_two, grad_shift_two, grad_bias_down]
    vectors += [grad_bias_query, grad_bias_value, *grad_bias_in, jnp.full((width,), count_local)]
    small = jnp.stack(vectors)
    small = jnp.pad(small, ((0, -small.shape[0] % 8), (0, 0)))
    outgoing = jnp.zeros((devices * capacity, width), BF16).at[slot_place].set(grad_embed.astype(BF16))
    summed, small, incoming = reduce_grads(grads, small, outgoing.reshape(devices, capacity, width), mp)
    group = summed
    for step in range(1, dp // INNER):
        shift = [(i, (i + step * INNER) % dp) for i in range(dp)]
        summed = (summed.astype(F32) + lax.ppermute(group, "dp", shift).astype(F32)).astype(BF16)
    summed = summed.reshape(BLOCKS, shard_rows, width)
    if dp > INNER:
        small = jnp.sum(lax.all_gather(small, "dp")[::INNER], axis=0)
    factor = lax.rsqrt(small[8 + mp, 0])
    small = small * factor
    gain_one_s, shift_one_s, bias_out_s, gain_two_s, shift_two_s, bias_down_s = (small[i] for i in range(6))
    m = lax.axis_index("mp")
    bias_query_s = small[6].reshape(mp, own_heads * HD)[m]
    bias_value_s = small[7].reshape(mp, own_heads * HD)[m]
    bias_in_s = small[8 : 8 + mp][m]
    grad_kinds = summed[0, :qkv_rows].reshape(3, own_heads, HD, width).transpose(3, 1, 0, 2).reshape(width, qkv_rows)
    received = jnp.where(slot_live[..., None], incoming.astype(F32), F32(0.0)).reshape(devices * capacity, width)
    grad_table = jnp.zeros(table.shape, F32).at[wanted_rows.reshape(-1)].add(received * factor)
    scaled = summed.astype(F32) * factor
    return (
        activations,
        grad_table,
        grad_kinds.astype(F32) * factor,
        bias_query_s,
        bias_value_s,
        scaled[0, qkv_rows:],
        bias_out_s,
        gain_one_s,
        shift_one_s,
        scaled[1],
        bias_in_s,
        scaled[2],
        bias_down_s,
        gain_two_s,
        shift_two_s,
    )


def solution(mesh):
    placed = (
        P(("dp", "mp"), None),
        P(("dp", "mp")),
        P(("dp", "mp")),
        P(),
        P(("dp", "mp"), None),
        P(None, "mp"),
        P("mp"),
        P("mp"),
        P("mp", None),
        P(),
        P(),
        P(),
        P(None, "mp"),
        P("mp"),
        P("mp", None),
        P(),
        P(),
        P(),
        P(("dp", "mp"), None),
    )
    return jax.shard_map(
        on_device,
        mesh=mesh,
        in_specs=placed,
        out_specs=(
            P(("dp", "mp"), None),
            P(("dp", "mp"), None),
            P(None, "mp"),
            P("mp"),
            P("mp"),
            P("mp", None),
            P(),
            P(),
            P(),
            P(None, "mp"),
            P("mp"),
            P("mp", None),
            P(),
            P(),
            P(),
        ),
        check_vma=False,
    )
```

```python
from functools import partial

import jax
import jax.numpy as jnp
from jax import lax
from jax.experimental import pallas as pl
from jax.experimental.pallas import tpu as pltpu
from jax.sharding import PartitionSpec as P

HD = 64
SEQ = 64
EPS = 1e-12
MESH = pl.DeviceIdType.MESH
F32 = jnp.float32
BF16 = jnp.bfloat16

INNER = 8
BLOCKS = 3


def position():
    d = lax.axis_index("dp")
    m = lax.axis_index("mp")
    core = lax.rem(d, 2)
    first = 4 - 2 * core
    second = 2 + 2 * core
    return d, m, first, second


def flip(d, bit):
    return d + bit - 2 * bit * lax.rem(lax.div(d, bit), 2)


def place(a, owner, piece, mp):
    if a == 0:
        return lax.div(piece, 2) * (2 * mp) + owner * 2 + lax.rem(piece, 2)
    return owner * INNER + piece


def nearest(m, mp):
    table = []
    for at in range(mp):
        owners = sorted((abs(o - at), o < at, (o - at) % mp) for o in range(mp) if o != at)
        table.append([entry[2] for entry in owners])
    offsets = []
    for i in range(mp - 1):
        k = table[0][i]
        for at in range(1, mp):
            k = jnp.where(m == at, table[at][i], k)
        offsets.append(k)
    return offsets


def enter_all(me, mp, devices):
    barrier = pltpu.get_barrier_semaphore()

    def greet(j, _):
        peer = lax.rem(me + j, devices)
        pl.semaphore_signal(
            barrier, inc=1, device_id=(lax.div(peer, mp), lax.rem(peer, mp)), device_id_type=MESH
        )
        return 0

    lax.fori_loop(1, devices, greet, 0)
    pl.semaphore_wait(barrier, devices - 1)


def remote(src, dst, send, recv, peer):
    return pltpu.make_async_remote_copy(
        src_ref=src, dst_ref=dst, send_sem=send, recv_sem=recv, device_id=peer, device_id_type=MESH
    )


def row_exchange(me, mp, devices, rows_ref, rows_out, send, recv, own_sem):
    def copy_to(j):
        peer = lax.rem(me + j, devices)
        return remote(
            rows_ref.at[peer], rows_out.at[me], send.at[j], recv.at[j], (lax.div(peer, mp), lax.rem(peer, mp))
        )

    def start():
        pltpu.make_async_copy(rows_ref.at[me], rows_out.at[me], own_sem).start()

        def body(j, _):
            copy_to(j).start()
            return 0

        lax.fori_loop(1, devices, body, 0)

    def finish():
        pltpu.make_async_copy(rows_ref.at[me], rows_out.at[me], own_sem).wait()

        def body(j, _):
            peer = lax.rem(me + devices - j, devices)
            back = remote(
                rows_ref.at[peer], rows_out.at[peer], send.at[j], recv.at[j], (lax.div(peer, mp), lax.rem(peer, mp))
            )
            back.wait_recv()
            back.wait_send()
            return 0

        lax.fori_loop(1, devices, body, 0)

    return start, finish


def gather_kernel(
    mp, devices, own_ref, bias_ref, rows_ref, out_ref, bias_out, rows_out, send, recv, z_send, own_sem, b_send, b_recv, r_send, r_recv
):
    d, m, first, second = position()
    me = d * mp + m
    enter_all(me, mp, devices)
    s = lax.rem(d, INNER)
    s1 = flip(s, first)
    s2 = flip(s, second)
    s3 = flip(s1, second)
    above = jnp.minimum(m + 1, mp - 1)
    below = jnp.maximum(m - 1, 0)

    def z_copy(a, owner, to, slot):
        at = out_ref.at[a, place(a, owner, s, mp)]
        k = lax.rem(owner - to + mp, mp)
        return remote(at, at, z_send.at[a, slot], recv.at[a, k, 0], (d, to))

    def own_z(a, to, slot):
        at = out_ref.at[a, place(a, m, s, mp)]
        k = lax.rem(m - to + mp, mp)
        return remote(own_ref.at[a, s], at, z_send.at[a, slot], recv.at[a, k, 0], (d, to))

    def start_own(a):
        @pl.when(m < mp - 1)
        def _():
            own_z(a, above, 0).start()

        @pl.when(m > 0)
        def _():
            own_z(a, below, 1).start()

    def own_copy(a, piece):
        return pltpu.make_async_copy(own_ref.at[a, piece], out_ref.at[a, place(a, m, piece, mp)], own_sem.at[a, piece])

    def bias_copy(k):
        return remote(bias_ref, bias_out.at[m], b_send.at[k], b_recv.at[mp - k], (d, lax.rem(m + k, mp)))

    start_rows, finish_rows = row_exchange(me, mp, devices, rows_ref, rows_out, r_send, r_recv, own_sem.at[BLOCKS, 0])
    for k in range(1, mp):
        bias_copy(k).start()
    bias_own = pltpu.make_async_copy(bias_ref, bias_out.at[m], own_sem.at[BLOCKS, 1])
    bias_own.start()
    start_own(0)
    start_rows()
    for a in range(1, BLOCKS):
        start_own(a)
    for a in range(BLOCKS):
        for piece in range(INNER):
            own_copy(a, piece).start()

    def hop(a, k, piece, slot, bit):
        ref = out_ref.at[a, place(a, lax.rem(m + k, mp), piece, mp)]
        return remote(ref, ref, send.at[a, k, slot], recv.at[a, k, slot], (flip(d, bit), m))

    offsets = nearest(m, mp)
    units = [(a, i) for a in range(BLOCKS) for i in range(mp - 1)]
    sent = []

    def go(copy):
        copy.start()
        sent.append(copy)

    def z_forward(a, i):
        owner = lax.rem(m + offsets[i], mp)
        return owner, z_copy(a, owner, below, 2 + i), z_copy(a, owner, above, 2 + i)

    for t in range(len(units) + 3):
        if t < len(units):
            a, i = units[t]
            k = offsets[i]
            owner, down, up = z_forward(a, i)
            remote(own_ref.at[a, s], out_ref.at[a, place(a, owner, s, mp)], send.at[a, k, 0], recv.at[a, k, 0], (d, owner)).wait_recv()

            @pl.when(jnp.logical_and(owner > m, m > 0))
            def _():
                down.start()

            @pl.when(jnp.logical_and(owner < m, m < mp - 1))
            def _():
                up.start()

            go(hop(a, k, s, 1, first))
            go(hop(a, k, s, 2, second))
            go(hop(a, k, s, 4, 1))
        if 0 <= t - 1 < len(units):
            a, i = units[t - 1]
            k = offsets[i]
            hop(a, k, s1, 1, first).wait_recv()
            go(hop(a, k, s1, 3, second))
            go(hop(a, k, s1, 5, 1))
        if 0 <= t - 2 < len(units):
            a, i = units[t - 2]
            k = offsets[i]
            hop(a, k, s2, 2, second).wait_recv()
            go(hop(a, k, s2, 6, 1))
            hop(a, k, s3, 3, second).wait_recv()
            go(hop(a, k, s3, 7, 1))
        if 0 <= t - 3 < len(units):
            a, i = units[t - 3]
            k = offsets[i]
            for slot, piece in ((4, s), (5, s1), (6, s2), (7, s3)):
                hop(a, k, flip(piece, 1), slot, 1).wait_recv()
    finish_rows()
    for k in range(1, mp):
        remote(bias_ref, bias_out.at[lax.rem(m + k, mp)], b_send.at[k], b_recv.at[k], (d, lax.rem(m + k, mp))).wait_recv()
        bias_copy(k).wait_send()
    bias_own.wait()
    for copy in sent:
        copy.wait_send()
    for a in range(BLOCKS):
        for piece in range(INNER):
            own_copy(a, piece).wait()

        @pl.when(m < mp - 1)
        def _():
            own_z(a, above, 0).wait_send()

        @pl.when(m > 0)
        def _():
            own_z(a, below, 1).wait_send()

        for i in range(mp - 1):
            owner, down, up = z_forward(a, i)

            @pl.when(jnp.logical_and(owner > m, m > 0))
            def _():
                down.wait_send()

            @pl.when(jnp.logical_and(owner < m, m < mp - 1))
            def _():
                up.wait_send()


def gather_weights(own, bias, rows, mp):
    _, inner, piece_rows, width = own.shape
    devices = rows.shape[0]
    vmem = pl.BlockSpec(memory_space=pltpu.VMEM)
    dma = pltpu.SemaphoreType.DMA
    return pl.pallas_call(
        partial(gather_kernel, mp, devices),
        out_shape=(
            jax.ShapeDtypeStruct((BLOCKS, mp * inner, piece_rows, width), BF16),
            jax.ShapeDtypeStruct((mp, *bias.shape), BF16),
            jax.ShapeDtypeStruct(rows.shape, BF16),
        ),
        in_specs=[vmem] * 3,
        out_specs=(vmem,) * 3,
        scratch_shapes=[
            dma((BLOCKS, mp, 8)),
            dma((BLOCKS, mp, 8)),
            dma((BLOCKS, 1 + mp)),
            dma((BLOCKS + 1, INNER)),
            dma((mp,)),
            dma((mp,)),
            dma((devices,)),
            dma((devices,)),
        ],
        compiler_params=pltpu.CompilerParams(
            collective_id=0, has_side_effects=True, vmem_limit_bytes=60 * 1024 * 1024
        ),
    )(own, bias, rows)


def reduce_kernel(
    mp,
    devices,
    grad_ref,
    small_ref,
    rows_ref,
    out_ref,
    small_out,
    rows_out,
    near,
    mid,
    far,
    line,
    part,
    part_in,
    send,
    recv,
    p_send,
    p_recv,
    r_send,
    r_recv,
    own_sem,
):
    d, m, first, second = position()
    me = d * mp + m
    enter_all(me, mp, devices)
    s = lax.rem(d, INNER)
    s1 = flip(s, first)
    s2 = flip(s, second)
    s3 = flip(s1, second)
    mine = (s, s1, s2, s3)
    other = tuple(flip(piece, 1) for piece in (s, s2, s1, s3))
    sent = []

    def go(copy):
        copy.start()
        sent.append(copy)

    units = [(a, k) for a in range(BLOCKS) for k in (*range(1, mp), 0)]

    def add(into, more):
        into[...] = (into[...].astype(F32) + more[...].astype(F32)).astype(BF16)

    def near_copy(a, k, i, owner):
        return remote(
            grad_ref.at[a, place(a, owner, other[i], mp)], near.at[a, k, i], send.at[a, k, i], recv.at[a, k, i], (flip(d, 1), m)
        )

    def mid_copy(a, k, i):
        return remote(
            near.at[a, k, 2 + i], mid.at[a, k, i], send.at[a, k, 4 + i], recv.at[a, k, 4 + i], (flip(d, second), m)
        )

    def far_copy(a, k):
        return remote(mid.at[a, k, 1], far.at[a, k], send.at[a, k, 6], recv.at[a, k, 6], (flip(d, first), m))

    def line_copy(a, k, owner):
        return remote(far.at[a, k], line.at[a, mp - k], send.at[a, k, 7], recv.at[a, mp - k, 7], (d, owner))

    def spread(a, i, piece, bit):
        ref = out_ref.at[a, piece]
        return remote(ref, ref, send.at[a, mp, i], recv.at[a, mp, i], (flip(d, bit), m))

    def part_copy(i):
        source = small_ref if i == 0 else part.at[i - 1]
        return remote(source, part_in.at[i], p_send.at[i], p_recv.at[i], (flip(d, 2**i), m))

    def total_copy(k):
        return remote(
            part.at[2], part_in.at[3 + m], p_send.at[2 + k], p_recv.at[3 + m], (d, lax.rem(m + k, mp))
        )

    def part_step(i):
        part_copy(i).wait_recv()
        part[i] = (small_ref[...] if i == 0 else part[i - 1]) + part_in[i]
        if i < 2:
            go(part_copy(i + 1))
        else:
            for k in range(1, mp):
                go(total_copy(k))

    start_rows, finish_rows = row_exchange(me, mp, devices, rows_ref, rows_out, r_send, r_recv, own_sem.at[0])
    go(part_copy(0))
    for n, (a, k) in enumerate(units):
        for i in (2, 3, 0, 1):
            go(near_copy(a, k, i, lax.rem(m + k, mp)))
        if n == 0:
            start_rows()
    for t in range(len(units) + 2):
        if t < len(units):
            a, k = units[t]
            owner = lax.rem(m + k, mp)
            for i in (2, 3, 0, 1):
                near_copy(a, k, i, owner).wait_recv()
                add(near.at[a, k, i], grad_ref.at[a, place(a, owner, mine[i], mp)])
                if i >= 2:
                    go(mid_copy(a, k, i - 2))
        if 0 <= t - 1 < len(units):
            a, k = units[t - 1]
            for i in (1, 0):
                mid_copy(a, k, i).wait_recv()
                add(mid.at[a, k, i], near.at[a, k, i])
                if i:
                    go(far_copy(a, k))
        if 0 <= t - 2 < len(units):
            a, k = units[t - 2]
            far_copy(a, k).wait_recv()
            add(far.at[a, k], mid.at[a, k, 0])
            if k:
                go(line_copy(a, k, lax.rem(m + k, mp)))
        if t in (2, 5, 8):
            part_step(t // 3)
    for a in range(BLOCKS):
        total = far[a, 0].astype(F32)
        for k in range(1, mp):
            remote(line.at[a, k], line.at[a, k], send.at[a, k, 7], recv.at[a, k, 7], (d, m)).wait_recv()
            total = total + line[a, k].astype(F32)
        out_ref[a, s] = total.astype(BF16)
        go(spread(a, 0, s, first))
        go(spread(a, 1, s, second))
        go(spread(a, 3, s, 1))
    for a in range(BLOCKS):
        spread(a, 0, s1, first).wait_recv()
        go(spread(a, 2, s1, second))
        go(spread(a, 4, s1, 1))
        spread(a, 1, s2, second).wait_recv()
        go(spread(a, 5, s2, 1))
    part_in[3 + m] = part[2]
    for k in range(1, mp):
        owner = lax.rem(m + k, mp)
        remote(part.at[2], part_in.at[3 + owner], p_send.at[2 + k], p_recv.at[3 + owner], (d, owner)).wait_recv()
    whole_sum = part_in[3]
    for k in range(1, mp):
        whole_sum = whole_sum + part_in[3 + k]
    small_out[...] = whole_sum
    for a in range(BLOCKS):
        spread(a, 2, s3, second).wait_recv()
        go(spread(a, 6, s3, 1))
    finish_rows()
    for a in range(BLOCKS):
        for i, piece in ((3, s), (4, s1), (5, s2), (6, s3)):
            spread(a, i, flip(piece, 1), 1).wait_recv()
    for copy in sent:
        copy.wait_send()


def reduce_grads(grads, small, rows, mp):
    blocks, pieces, piece_rows, width = grads.shape
    devices = rows.shape[0]
    vmem = pl.BlockSpec(memory_space=pltpu.VMEM)
    dma = pltpu.SemaphoreType.DMA
    return pl.pallas_call(
        partial(reduce_kernel, mp, devices),
        out_shape=(
            jax.ShapeDtypeStruct((blocks, pieces // mp, piece_rows, width), BF16),
            jax.ShapeDtypeStruct(small.shape, F32),
            jax.ShapeDtypeStruct(rows.shape, BF16),
        ),
        in_specs=[vmem] * 3,
        out_specs=(vmem,) * 3,
        scratch_shapes=[
            pltpu.VMEM((blocks, mp, 4, piece_rows, width), BF16),
            pltpu.VMEM((blocks, mp, 2, piece_rows, width), BF16),
            pltpu.VMEM((blocks, mp, piece_rows, width), BF16),
            pltpu.VMEM((blocks, mp, piece_rows, width), BF16),
            pltpu.VMEM((3, *small.shape), F32),
            pltpu.VMEM((3 + mp, *small.shape), F32),
            dma((blocks, mp + 1, 8)),
            dma((blocks, mp + 1, 8)),
            dma((2 + mp,)),
            dma((3 + mp,)),
            dma((devices,)),
            dma((devices,)),
            dma((1,)),
        ],
        compiler_params=pltpu.CompilerParams(
            collective_id=1, has_side_effects=True, vmem_limit_bytes=63 * 1024 * 1024
        ),
    )(grads, small, rows)


NN = (((1,), (0,)), ((), ()))
NT = (((1,), (1,)), ((), ()))
TN = (((0,), (0,)), ((), ()))
ROOT_HALF = 0.7071067811865476
DENSITY = 0.3989422804014327


def mul(lhs, rhs, dims):
    return lax.dot_general(lhs, rhs, dims, preferred_element_type=F32)


def row_mean(v):
    return jnp.mean(v, axis=1, keepdims=True)


def column_sum(v):
    return jnp.sum(v, axis=0, keepdims=True)


def norm_rows(hidden, gain_vec, shift_vec):
    centred = hidden - row_mean(hidden)
    row_scale = lax.rsqrt(row_mean(centred * centred) + EPS)
    normed = centred * row_scale
    return normed * gain_vec + shift_vec, normed, row_scale


def norm_back(grad_out, normed, row_scale, gain_vec):
    grad_normed = grad_out * gain_vec
    return row_scale * (grad_normed - row_mean(grad_normed) - normed * row_mean(grad_normed * normed))


def layer_kernel(
    mp,
    slot_col,
    slot_row,
    weight_col,
    live_col,
    rows_ref,
    w_ref,
    bias_ref,
    bias_in_ref,
    vec_ref,
    cot_ref,
    count_ref,
    act_out,
    grad_ref,
    small_ref,
    rows_out,
    emb,
    qkv,
    probs,
    ctx,
    first,
    normed,
    first_low,
    acc,
    act,
    slope,
    grad_low,
    grad_qkv,
    acc_two,
):
    tokens, width = act_out.shape
    slots = rows_ref.shape[0]
    per_kind = 2 * mp
    pairs = width // 128

    def weight(a, at, number):
        return w_ref[a, pl.ds(at, number)].reshape(width, width)

    def put(a, at, number, value):
        grad_ref[a, pl.ds(at, number)] = value.astype(BF16).reshape(number, width // number, width)

    def vec(i):
        return vec_ref[i : i + 1, :]

    pick = (lax.broadcasted_iota(jnp.int32, (tokens, slots), 1) == slot_col[...]).astype(F32).astype(BF16)
    emb[...] = mul(pick, rows_ref[...], NN).astype(BF16)

    def project(j, _):
        qkv[j] = (mul(emb[...], weight(0, j * per_kind, per_kind), NT) + bias_ref[j]).astype(BF16)
        return 0

    lax.fori_loop(0, 3, project, 0)

    low_half = lax.broadcasted_iota(jnp.int32, (1, 128), 1) < HD

    def halves(v):
        zero = jnp.zeros_like(v)
        return jnp.where(low_half, v, zero), jnp.where(low_half, zero, v)

    def lanes(pair):
        return pl.ds(pl.multiple_of(pair * 128, 128), 128)

    def attend(pair, _):
        key_sent = lax.div(lax.broadcasted_iota(jnp.int32, (tokens, tokens), 0), SEQ)
        query_sent = lax.div(lax.broadcasted_iota(jnp.int32, (tokens, tokens), 1), SEQ)
        seen = jnp.logical_and(key_sent == query_sent, live_col[...] > 0.0)
        keys = qkv[1, :, lanes(pair)]
        values = qkv[2, :, lanes(pair)]
        parts = []
        for half, queries in enumerate(halves(qkv[0, :, lanes(pair)])):
            scores = jnp.where(seen, mul(keys, queries, NT) * 0.125, F32(-1e30))
            weights = jnp.exp(scores - jnp.max(scores, axis=0, keepdims=True))
            weights = weights / column_sum(weights)
            probs[2 * pair + half] = weights
            parts.append(mul(weights.astype(BF16), values, TN))
        ctx[:, lanes(pair)] = jnp.where(low_half, parts[0], parts[1]).astype(BF16)
        return 0

    lax.fori_loop(0, pairs, attend, 0)

    hidden = emb[...].astype(F32) + mul(ctx[...], weight(0, 3 * per_kind, per_kind), NN) + vec(2)
    first_value, normed_one, scale_one = norm_rows(hidden, vec(0), vec(1))
    first[...] = first_value
    normed[...] = normed_one
    first_low[...] = first_value.astype(BF16)
    acc[...] = first_value + vec(5)

    def feed(m, _):
        pre = mul(first_low[...], weight(1, m * INNER, INNER), NN) + bias_in_ref[m]
        half_gate = 0.5 + 0.5 * lax.erf(pre * ROOT_HALF)
        act[m] = (pre * half_gate).astype(BF16)
        slope[m] = half_gate + pre * (jnp.exp(-0.5 * pre * pre) * DENSITY)
        acc[...] += mul(act[m], weight(2, m * INNER, INNER), NN)
        return 0

    lax.fori_loop(0, mp, feed, 0)

    final, normed_two, scale_two = norm_rows(acc[...], vec(3), vec(4))
    act_out[...] = final.astype(BF16)
    grad_final = weight_col[...] * cot_ref[...].astype(F32)
    small_ref[3:4, :] = column_sum(grad_final * normed_two)
    small_ref[4:5, :] = column_sum(grad_final)
    grad_h2 = norm_back(grad_final, normed_two, scale_two, vec(3))
    small_ref[5:6, :] = column_sum(grad_h2)
    grad_low[...] = grad_h2.astype(BF16)
    acc[...] = grad_h2

    def feed_back(m, _):
        put(2, m * INNER, INNER, mul(act[m], grad_low[...], TN))
        grad_pre = mul(grad_low[...], weight(2, m * INNER, INNER), NT) * slope[m]
        low = grad_pre.astype(BF16)
        small_ref[pl.ds(8 + m, 1), :] = column_sum(low.astype(F32))
        put(1, m * INNER, INNER, mul(first_low[...], low, TN))
        acc[...] += mul(low, weight(1, m * INNER, INNER), NT)
        return 0

    lax.fori_loop(0, mp, feed_back, 0)

    grad_first = acc[...]
    small_ref[0:1, :] = column_sum(grad_first * normed[...])
    small_ref[1:2, :] = column_sum(grad_first)
    grad_h1 = norm_back(grad_first, normed[...], scale_one, vec(0))
    small_ref[2:3, :] = column_sum(grad_h1)
    acc_two[...] = grad_h1
    grad_attn = grad_h1.astype(BF16)
    put(0, 3 * per_kind, per_kind, mul(ctx[...], grad_attn, TN))
    grad_low[...] = mul(grad_attn, weight(0, 3 * per_kind, per_kind), NT).astype(BF16)

    def attend_back(pair, _):
        queries = qkv[0, :, lanes(pair)]
        keys = qkv[1, :, lanes(pair)]
        values = qkv[2, :, lanes(pair)]
        grad_ctx = grad_low[:, lanes(pair)]
        parts = []
        for half, masked in enumerate(halves(grad_ctx)):
            weights = probs[2 * pair + half]
            grad_probs = mul(values, masked, NT)
            grad_scores = weights * (grad_probs - column_sum(grad_probs * weights))
            grad_scores = grad_scores.astype(BF16)
            parts.append(
                (
                    mul(grad_scores, keys, TN) * 0.125,
                    mul(grad_scores, queries, NN) * 0.125,
                    mul(weights.astype(BF16), grad_ctx, NN),
                )
            )
        for j in range(3):
            grad_qkv[j, :, lanes(pair)] = jnp.where(low_half, parts[0][j], parts[1][j]).astype(BF16)
        return 0

    lax.fori_loop(0, pairs, attend_back, 0)

    def project_back(j, _):
        put(0, j * per_kind, per_kind, mul(grad_qkv[j], emb[...], TN))
        acc_two[...] += mul(grad_qkv[j], weight(0, j * per_kind, per_kind), NN)
        return 0

    lax.fori_loop(0, 3, project_back, 0)
    small_ref[6:7, :] = column_sum(grad_qkv[0].astype(F32))
    small_ref[7:8, :] = column_sum(grad_qkv[2].astype(F32))
    small_ref[8 + mp :, :] = jnp.broadcast_to(count_ref[...], (small_ref.shape[0] - 8 - mp, width))
    unpick = (lax.broadcasted_iota(jnp.int32, (slots, tokens), 0) == slot_row[...]).astype(F32).astype(BF16)
    rows_out[...] = mul(unpick, acc_two[...].astype(BF16), NN).astype(BF16)


def layer(mp, slot_place, row_weight, token_live, rows, whole, bias_qkv, bias_in, vectors, cotangent, count):
    tokens, width = cotangent.shape
    heads = width // HD
    vmem = pl.BlockSpec(memory_space=pltpu.VMEM)
    small_rows = -(-(9 + mp) // 8) * 8
    return pl.pallas_call(
        partial(layer_kernel, mp),
        out_shape=(
            jax.ShapeDtypeStruct((tokens, width), BF16),
            jax.ShapeDtypeStruct(whole.shape, BF16),
            jax.ShapeDtypeStruct((small_rows, width), F32),
            jax.ShapeDtypeStruct(rows.shape, BF16),
        ),
        in_specs=[vmem] * 11,
        out_specs=(vmem,) * 4,
        scratch_shapes=[
            pltpu.VMEM((tokens, width), BF16),
            pltpu.VMEM((3, tokens, width), BF16),
            pltpu.VMEM((heads, tokens, tokens), F32),
            pltpu.VMEM((tokens, width), BF16),
            pltpu.VMEM((tokens, width), F32),
            pltpu.VMEM((tokens, width), F32),
            pltpu.VMEM((tokens, width), BF16),
            pltpu.VMEM((tokens, width), F32),
            pltpu.VMEM((mp, tokens, width), BF16),
            pltpu.VMEM((mp, tokens, width), F32),
            pltpu.VMEM((tokens, width), BF16),
            pltpu.VMEM((3, tokens, width), BF16),
            pltpu.VMEM((tokens, width), F32),
        ],
        compiler_params=pltpu.CompilerParams(vmem_limit_bytes=62 * 1024 * 1024),
    )(
        slot_place.reshape(tokens, 1),
        slot_place.reshape(1, tokens),
        row_weight.reshape(tokens, 1),
        token_live.reshape(tokens, 1),
        rows,
        whole,
        bias_qkv,
        bias_in,
        vectors,
        cotangent,
        count,
    )


def on_device(
    token_block,
    token_offset,
    lengths,
    group_counts,
    table,
    weight_qkv,
    bias_query,
    bias_value,
    weight_out,
    bias_out,
    gain_one,
    shift_one,
    weight_in,
    bias_in,
    weight_down,
    bias_down,
    gain_two,
    shift_two,
    cotangent,
):
    axes = ("dp", "mp")
    devices = lax.axis_size(axes)
    mp = lax.axis_size("mp")
    dp = lax.axis_size("dp")
    me = lax.axis_index(axes)
    tok_rows = token_offset.shape[0]
    width = table.shape[1]
    sent_local = lengths.shape[0]
    shard_rows = weight_down.shape[0]
    qkv_rows = weight_qkv.shape[1]
    own_heads = qkv_rows // (3 * HD)
    slice_rows = shard_rows // INNER

    kinds = weight_qkv.reshape(width, own_heads, 3, HD).transpose(2, 1, 3, 0).reshape(qkv_rows, width)
    own = jnp.stack([jnp.concatenate([kinds, weight_out], axis=0), weight_in, weight_down])
    bias_own = jnp.concatenate([bias_query, bias_value, bias_in])
    bias_rows = bias_own.shape[0] // 128
    bias_own = jnp.pad(bias_own.reshape(bias_rows, 128), ((0, -bias_rows % 16), (0, 0)))

    capacity = max(2, 2 * tok_rows // devices)
    token_owner = token_block[:, 0]
    owner_hits = (token_owner[:, None] == jnp.arange(devices, dtype=jnp.int32)[None, :]).astype(jnp.int32)
    slot_index = jnp.sum((jnp.cumsum(owner_hits, axis=0) - 1) * owner_hits, axis=1)
    slot_place = token_owner * capacity + slot_index
    requests = jnp.full((devices * capacity,), -1, jnp.int32).at[slot_place].set(token_offset)
    wanted = lax.all_to_all(requests.reshape(devices, capacity), axes, split_axis=0, concat_axis=0, tiled=True)
    slot_live = wanted >= 0
    wanted_rows = jnp.maximum(wanted, 0)
    whole, bias_all, fetched = gather_weights(
        own.reshape(BLOCKS, INNER, slice_rows, width), bias_own, table[wanted_rows], mp
    )
    bias_all = bias_all.reshape(mp, -1).astype(F32)
    b_query = bias_all[:, : own_heads * HD].reshape(1, width)
    b_value = bias_all[:, own_heads * HD : 2 * own_heads * HD].reshape(1, width)
    b_in = bias_all[:, 2 * own_heads * HD : 2 * own_heads * HD + bias_in.shape[0]].reshape(mp, 1, width)
    bias_qkv = jnp.stack([b_query, jnp.zeros_like(b_query), b_value])

    total_sent = sent_local * devices
    group_num = group_counts.shape[0]
    sent_index = me * sent_local + jnp.arange(sent_local, dtype=jnp.int32)
    offsets = jnp.cumsum(group_counts) - group_counts
    member = (sent_index[:, None] >= offsets[None, :]) & (sent_index[:, None] < (offsets + group_counts)[None, :])
    group_weight = total_sent / (group_num * group_counts.astype(F32))
    sent_weight = jnp.sum(jnp.where(member, group_weight[None, :], F32(0.0)), axis=1)
    positions = jnp.arange(SEQ, dtype=jnp.int32)
    token_live = (positions[None, :] < lengths[:, None]).astype(F32)
    row_weight = (token_live * sent_weight[:, None]).reshape(tok_rows)
    count_local = jnp.sum(lengths).astype(F32)

    vectors = jnp.stack([gain_one, shift_one, bias_out, gain_two, shift_two, bias_down]).astype(F32)
    activations, grads, small, outgoing = layer(
        mp,
        slot_place,
        row_weight,
        token_live,
        fetched.reshape(devices * capacity, width),
        whole,
        bias_qkv,
        b_in,
        vectors,
        cotangent,
        count_local.reshape(1, 1),
    )
    summed, small, incoming = reduce_grads(grads, small, outgoing.reshape(devices, capacity, width), mp)
    group = summed
    for step in range(1, dp // INNER):
        shift = [(i, (i + step * INNER) % dp) for i in range(dp)]
        summed = (summed.astype(F32) + lax.ppermute(group, "dp", shift).astype(F32)).astype(BF16)
    summed = summed.reshape(BLOCKS, shard_rows, width)
    if dp > INNER:
        small = jnp.sum(lax.all_gather(small, "dp")[::INNER], axis=0)
    factor = lax.rsqrt(small[8 + mp, 0])
    small = small * factor
    gain_one_s, shift_one_s, bias_out_s, gain_two_s, shift_two_s, bias_down_s = (small[i] for i in range(6))
    m = lax.axis_index("mp")
    bias_query_s = small[6].reshape(mp, own_heads * HD)[m]
    bias_value_s = small[7].reshape(mp, own_heads * HD)[m]
    bias_in_s = small[8 : 8 + mp][m]
    grad_kinds = summed[0, :qkv_rows].reshape(3, own_heads, HD, width).transpose(3, 1, 0, 2).reshape(width, qkv_rows)
    received = jnp.where(slot_live[..., None], incoming.astype(F32), F32(0.0)).reshape(devices * capacity, width)
    grad_table = jnp.zeros(table.shape, F32).at[wanted_rows.reshape(-1)].add(received * factor)
    scaled = summed.astype(F32) * factor
    return (
        activations,
        grad_table,
        grad_kinds.astype(F32) * factor,
        bias_query_s,
        bias_value_s,
        scaled[0, qkv_rows:],
        bias_out_s,
        gain_one_s,
        shift_one_s,
        scaled[1],
        bias_in_s,
        scaled[2],
        bias_down_s,
        gain_two_s,
        shift_two_s,
    )


def solution(mesh):
    placed = (
        P(("dp", "mp"), None),
        P(("dp", "mp")),
        P(("dp", "mp")),
        P(),
        P(("dp", "mp"), None),
        P(None, "mp"),
        P("mp"),
        P("mp"),
        P("mp", None),
        P(),
        P(),
        P(),
        P(None, "mp"),
        P("mp"),
        P("mp", None),
        P(),
        P(),
        P(),
        P(("dp", "mp"), None),
    )
    return jax.shard_map(
        on_device,
        mesh=mesh,
        in_specs=placed,
        out_specs=(
            P(("dp", "mp"), None),
            P(("dp", "mp"), None),
            P(None, "mp"),
            P("mp"),
            P("mp"),
            P("mp", None),
            P(),
            P(),
            P(),
            P(None, "mp"),
            P("mp"),
            P("mp", None),
            P(),
            P(),
            P(),
        ),
        check_vma=False,
    )
```
